256 devices in a mesh: rows: 64 (over z_hi, y, x, core), lags: 4 (over z_lo).
Axes of the slice: x: 4, y: 4, z: 8 (z_hi: 2, z_lo: 4; z = z_hi * 4 + z_lo), core: 2. Of those that a mesh axis runs over, the one named last changes fastest.
Arguments:
- history: float32 [32, 16, 16384], P('lags', None, 'rows'), may hold values from -6 to 6
- incident: float32 [2, 16, 16384], P(None, None, 'rows'), may hold values from -6 to 6
- kernel: float32 [64, 32, 6, 256, 256], P('rows', 'lags'), may hold values from -0.02734375 to 0.02734375
- near_blocks: int32 [64, 32, 6], P('rows', 'lags'), may hold values from 0 to 63, as said below
- self_inverse: float32 [64, 256, 256], P('rows'), may hold values from -1 to 1
Outputs:
- densities: float32 [2, 16, 16384], P(None, None, 'rows')
The draws below stay inside these ranges and needn't reach their ends.
Inputs may be any that keep to these rules, and one draw needn't show every extreme that they name: `near_blocks`: indices of source blocks; for each row block and each group of 8 consecutive lags, no source block appears more than 1 times among its 48 entries, and some block appears exactly 1 times.
All inputs are finite; a program needn't handle non-finite values.
Results may differ from the reference program's by a relative error of at most 0.00012.
Values sent between devices are 32-bit elements; how exact they have to be, the bound alone decides.
No kernel may reach another device: no remote copies, remote signals or barrier semaphores. Data moves between devices by JAX's collectives and lax.ppermute only.
A program may use at most 128 MiB of HBM per device.

```python
import math
import jax
import jax.numpy as jnp
from jax import lax

BLOCK = 256
W = 16
LAG_DEV = 8
NEAR = 6
STEPS = 2
LAGS = 32
NB = 64
N = 16384
MOST = 1


def draw_self_inverse(key, part):
    spread = 0.3 / math.sqrt(BLOCK)
    noise = spread * jax.random.truncated_normal(key, -4.0, 4.0, (NB, BLOCK, BLOCK), jnp.float32)
    return noise + 0.5 * jnp.eye(BLOCK, dtype=jnp.float32)[None]


def draw_near_blocks(key, part):
    groups = LAGS // LAG_DEV
    slot_total = LAG_DEV * NEAR
    base = jax.random.fold_in(key, 7)

    def one_group(group_key):
        first_key, second_key = jax.random.split(group_key)
        perm_keys = jax.random.split(first_key, MOST)
        perms = jax.vmap(lambda inner: jax.random.permutation(inner, NB))(perm_keys)
        listed = perms.reshape(MOST * NB)[:slot_total].astype(jnp.int32)
        return jax.random.permutation(second_key, listed)
    group_keys = jax.random.split(base, NB * groups)
    drawn = jax.vmap(one_group)(group_keys)
    return drawn.reshape(NB, groups * LAG_DEV, NEAR).astype(jnp.int32)


def levels(rng, extent, cuts, smallest, top_value):
    def one(position, parts):
        heights = jax.random.uniform(jax.random.fold_in(jax.random.fold_in(rng, 6), position), (parts,), jnp.float32, smallest / len(cuts), top_value / len(cuts))
        return jnp.repeat(jnp.exp(heights), extent[position] // parts).reshape((-1,) + (1,) * (len(extent) - position - 1))

    level = one(*cuts[0])
    for cut in cuts[1:]:
        level = level * one(*cut)
    return level


def bell_draw(own_key, shape, scale, most, cuts=(), kind=jnp.bfloat16):
    entries = jax.random.normal(own_key, shape, jnp.float32) * scale
    if len(cuts) > 0:
        entries = levels(own_key, shape, cuts, -0.22, 0.18) * entries
    return jnp.clip(entries, min=-most, max=most).astype(kind)


def setup_inputs(seed: int = 0) -> dict:
    key_of = jax.random.split(jax.random.key(seed), 6)
    return {
        "history": bell_draw(key_of[0], (LAGS, W, N), 0.7, 6.0, ((0, 4), (2, 64)), jnp.float32),
        "incident": bell_draw(key_of[1], (STEPS, W, N), 1.0, 6.0, ((2, 64),), jnp.float32),
        "kernel": bell_draw(key_of[2], (NB, LAGS, NEAR, BLOCK, BLOCK), (NEAR * LAGS * BLOCK) ** -0.5, 0.02734375, ((0, 64), (1, 4)), jnp.float32),
        "near_blocks": draw_near_blocks(jax.random.fold_in(key_of[5], 71), 0),
        "self_inverse": draw_self_inverse(jax.random.fold_in(key_of[5], 71), 0),
    }


def reference(history, incident, kernel, near_blocks, self_inverse):
    highest = lax.Precision.HIGHEST
    past_window = history.reshape(LAGS, W, NB, BLOCK)
    outputs = []
    for instant in range(STEPS):
        def one_block(operands):
            kernel_rows, source_ids = operands
            lag_index = jnp.arange(LAGS, dtype=jnp.int32)[:, None]
            picked = past_window[lag_index, :, source_ids]
            return jnp.einsum("lkwc,lkcr->wr", picked, kernel_rows, precision=highest)

        fields = lax.map(one_block, (kernel, near_blocks))
        near_field = jnp.transpose(fields, (1, 0, 2))
        driven = incident[instant].reshape(W, NB, BLOCK) - near_field
        density = jnp.einsum("wic,icr->wir", driven, self_inverse, precision=highest)
        outputs.append(density.reshape(W, NB * BLOCK))
        past_window = jnp.concatenate([density[None], past_window[:-1]], axis=0)
    return jnp.stack(outputs)
```

```python
import jax
import jax.numpy as jnp
from jax import lax
from jax.experimental import pallas as pl
from jax.experimental.pallas import tpu as pltpu
from jax.sharding import Mesh
from jax.sharding import PartitionSpec as P

PLANE = ("y", "x", "core")
ROWS = ("z_hi",) + PLANE
F32 = jnp.float32
BF16 = jnp.bfloat16


def split(value):
    high = value.astype(BF16)
    low = (value - high.astype(F32)).astype(BF16)
    return high, low


def product(left, right):
    waves = left.shape[0]
    left_high, left_low = split(left)
    right_high, right_low = split(right)
    both = jnp.concatenate([left_high, left_low], axis=0)
    first = jnp.dot(both, right_high, preferred_element_type=F32)
    second = jnp.dot(left_high, right_low, preferred_element_type=F32)
    return first[:waves] + (first[waves:] + second)


def pack(table, own, twin, shift):
    peers, planes = table.shape
    block = own.shape[1:]

    def body(table_ref, own_ref, twin_ref, out_ref):
        for peer in range(peers):
            out_ref[peer, 0] = own_ref[table_ref[peer, 0] + shift]
            out_ref[peer, 1] = twin_ref[table_ref[peer, 1] + shift]

    vmem = pl.BlockSpec(memory_space=pltpu.VMEM)
    return pl.pallas_call(
        body,
        out_shape=jax.ShapeDtypeStruct((peers, planes) + block, F32),
        in_specs=[pl.BlockSpec(memory_space=pltpu.SMEM), vmem, vmem],
        out_specs=vmem,
        name=f"pack{shift}",
    )(table, own, twin)


def near_partial(ids, received, kernel, name):
    lag_dev, near, size, _ = kernel.shape
    peers, planes, waves, _ = received.shape

    def body(ids_ref, received_ref, kernel_ref, out_ref):
        lag = pl.program_id(0)
        total = jnp.zeros((waves, size), F32)
        for slot in range(near):
            source = ids_ref[lag, slot]
            block = received_ref[source % peers, source // peers]
            total = total + product(block, kernel_ref[0, slot])

        @pl.when(lag == 0)
        def _():
            out_ref[...] = total

        @pl.when(lag > 0)
        def _():
            out_ref[...] += total

    return pl.pallas_call(
        body,
        grid=(lag_dev,),
        out_shape=jax.ShapeDtypeStruct((waves, size), F32),
        in_specs=[
            pl.BlockSpec(memory_space=pltpu.SMEM),
            pl.BlockSpec(memory_space=pltpu.VMEM),
            pl.BlockSpec((1, near, size, size), lambda lag: (lag, 0, 0, 0)),
        ],
        out_specs=pl.BlockSpec((waves, size), lambda lag: (0, 0)),
        name=name,
    )(ids, received, kernel)


def first_density(plane, partials, incident, twin_incident, inverse, twin_inverse):
    groups = partials.shape[0] // 2
    waves, size = incident.shape

    def body(plane_ref, partials_ref, inc_ref, twin_inc_ref, inv_ref, twin_inv_ref, out_ref):
        own = plane_ref[0] * groups
        twin = groups - own
        near = partials_ref[own]
        twin_near = partials_ref[twin]
        for group in range(1, groups):
            near = near + partials_ref[own + group]
            twin_near = twin_near + partials_ref[twin + group]
        out_ref[0] = product(inc_ref[...] - near, inv_ref[...])
        out_ref[1] = product(twin_inc_ref[...] - twin_near, twin_inv_ref[...])

    vmem = pl.BlockSpec(memory_space=pltpu.VMEM)
    return pl.pallas_call(
        body,
        out_shape=jax.ShapeDtypeStruct((2, waves, size), F32),
        in_specs=[pl.BlockSpec(memory_space=pltpu.SMEM)] + [vmem] * 5,
        out_specs=vmem,
        name="first_density",
    )(plane, partials, incident, twin_incident, inverse, twin_inverse)


def last_density(ids, core, mine, partner, kernel, driven, inverse):
    near, size, _ = kernel.shape
    waves = driven.shape[0]

    def body(ids_ref, core_ref, mine_ref, partner_ref, kernel_ref, driven_ref, inv_ref, out_ref):
        total = jnp.zeros((waves, size), F32)
        for slot in range(near):
            source = ids_ref[slot]
            chip = (source // 2) % 16
            plane = source // 32
            same = (source % 2) == core_ref[0]
            block = jnp.where(same, mine_ref[chip, plane], partner_ref[chip, plane])
            total = total + product(block, kernel_ref[slot])
        out_ref[...] = product(driven_ref[...] - total, inv_ref[...])

    vmem = pl.BlockSpec(memory_space=pltpu.VMEM)
    smem = pl.BlockSpec(memory_space=pltpu.SMEM)
    return pl.pallas_call(
        body,
        out_shape=jax.ShapeDtypeStruct((waves, size), F32),
        in_specs=[smem, smem] + [vmem] * 5,
        out_specs=vmem,
        name="last_density",
    )(ids, core, mine, partner, kernel, driven, inverse)


def shards(history, incident, kernel, near_blocks, self_inverse):
    lag_dev, waves, size = history.shape
    kernel_rows = kernel[0]
    inverse = self_inverse[0]
    near = near_blocks.shape[2]
    planes = lax.axis_size("z_hi")
    peers = lax.axis_size(PLANE)
    groups = lax.axis_size("lags")
    plane = lax.axis_index("z_hi")
    core = lax.axis_index("core")
    swap = [(0, 1), (1, 0)]

    before = lax.ppermute(history[lag_dev - 1], "lags", [(g, g + 1) for g in range(groups - 1)])
    window = jnp.concatenate([before[None], history], axis=0)
    twin_window = lax.ppermute(window, "z_hi", swap)
    twin_inverse = lax.ppermute(inverse, "z_hi", swap)
    twin_incident = lax.ppermute(incident[0], "z_hi", swap)

    ids = jnp.bitwise_xor(near_blocks[0], plane * peers)
    hit = ids.reshape(lag_dev * near, 1) == jnp.arange(planes * peers, dtype=jnp.int32)[None, :]
    lag_of = jnp.repeat(jnp.arange(lag_dev, dtype=jnp.int32), near)[:, None]
    wanted = jnp.sum(jnp.where(hit, lag_of, 0), axis=0)
    wanted = jnp.pad(wanted.reshape(planes, peers).T[:, None, :], ((0, 0), (0, 0), (0, 128 - planes)))
    table = lax.all_to_all(wanted, PLANE, 0, 0, tiled=True)[:, 0, :planes]

    received0 = lax.all_to_all(pack(table, window, twin_window, 1), PLANE, 0, 0, tiled=True)
    received1 = lax.all_to_all(pack(table, window, twin_window, 0), PLANE, 0, 0, tiled=True)

    partial0 = near_partial(ids, received0, kernel_rows, "near0")
    spread = jnp.broadcast_to(partial0[None], (planes * groups, waves, size))
    partials = lax.all_to_all(spread, ("z_hi", "lags"), 0, 0, tiled=True)
    density0 = first_density(plane[None], partials, incident[0], twin_incident, inverse, twin_inverse)

    chips = peers // 2
    spread = jnp.broadcast_to(density0[None], (chips, planes, waves, size))
    mine = lax.all_to_all(spread, ("y", "x"), 0, 0, tiled=True)
    partner = lax.ppermute(mine, "core", swap)

    partial1 = near_partial(ids, received1, kernel_rows, "near1")
    driven = incident[1] - partial1
    for group in range(1, groups):
        driven = driven - lax.ppermute(partial1, "lags", [(group, 0)])

    density1 = last_density(ids[0], core[None], mine, partner, kernel_rows[0], driven, inverse)
    result = jnp.where(lax.axis_index("lags") == 0, density1, 0.0)
    for group in range(1, groups):
        result = result + lax.ppermute(density1, "lags", [(0, group)])
    return jnp.stack([density0[0], result])


def solution(mesh):
    shape = (2, 4, 4, 2, mesh.shape["lags"])
    parts = Mesh(mesh.devices.reshape(shape), ROWS + ("lags",))
    in_specs = (
        P("lags", None, ROWS),
        P(None, None, ROWS),
        P(ROWS, "lags", None, None, None),
        P(ROWS, "lags", None),
        P(ROWS, None, None),
    )
    out_specs = P(None, None, ROWS)
    return jax.shard_map(shards, mesh=parts, in_specs=in_specs, out_specs=out_specs, check_vma=False)
```

```python
import jax
import jax.numpy as jnp
from jax import lax
from jax.experimental import pallas as pl
from jax.experimental.pallas import tpu as pltpu
from jax.sharding import Mesh
from jax.sharding import PartitionSpec as P


PLANE = ("y", "x", "core")
ROWS = ("z_hi",) + PLANE
F32 = jnp.float32
BF16 = jnp.bfloat16
VMEM = pl.BlockSpec(memory_space=pltpu.VMEM)
SMEM = pl.BlockSpec(memory_space=pltpu.SMEM)
PARAMS = pltpu.CompilerParams(vmem_limit_bytes=8 << 20)


def resident(array):
    return pltpu.with_memory_space_constraint(array, pltpu.VMEM)


def call(body, out, in_specs, operands, aliases=None):
    held = [resident(a) if s is VMEM else a for a, s in zip(operands, in_specs)]
    return pl.pallas_call(
        body,
        out_shape=out,
        in_specs=in_specs,
        out_specs=jax.tree.map(lambda _: VMEM, out),
        input_output_aliases=aliases or {},
        compiler_params=PARAMS,
    )(*held)


def split(value):
    high = value.astype(BF16)
    low = (value - high.astype(F32)).astype(BF16)
    return high, low


def product(left, right_high, right_low):
    waves = left.shape[0]
    left_high, left_low = split(left)
    both = jnp.concatenate([left_high, left_low], axis=0)
    first = jnp.dot(both, right_high, preferred_element_type=F32)
    second = jnp.dot(left_high, right_low, preferred_element_type=F32)
    return first[:waves] + (first[waves:] + second)


def lag_table(near_t, base, peers, lanes):
    near, _, lag_dev = near_t.shape

    def body(near_ref, base_ref, out_ref):
        ids = lax.broadcasted_iota(jnp.int32, (peers, lanes), 1) * peers
        ids = ids + lax.broadcasted_iota(jnp.int32, (peers, lanes), 0)
        table = jnp.zeros((peers, lanes), jnp.int32)
        for slot in range(near):
            for lag in range(1, lag_dev):
                source = jnp.bitwise_xor(near_ref[slot, 0, lag], base_ref[0])
                table = jnp.where(ids == source, lag, table)
        out_ref[...] = table

    return call(body, jax.ShapeDtypeStruct((peers, lanes), jnp.int32), [SMEM, SMEM], [near_t, base])


def pack(table, own, twin, before, twin_before):
    peers, _, _ = table.shape
    block = own.shape[1:]
    out = pltpu.VMEM((peers, 2, 2) + block, F32)

    def body(table_ref, own_ref, twin_ref, before_ref, twin_before_ref, out_ref):
        edges = (before_ref[...], twin_before_ref[...])
        for peer in range(peers):
            for plane, ref in enumerate((own_ref, twin_ref)):
                lag = table_ref[peer, 0, plane]
                out_ref[peer, 0, plane] = ref[lag]
                nearer = ref[jnp.maximum(lag - 1, 0)]
                out_ref[peer, 1, plane] = jnp.where(lag == 0, edges[plane], nearer)

    return call(body, out, [SMEM] + [VMEM] * 4, [table, own, twin, before, twin_before])


def split_kernel(kernel):
    lag_dev, near, size, _ = kernel.shape

    def body(kernel_ref, high_ref, low_ref, first_high_ref, first_low_ref):
        lag = pl.program_id(0)
        high, low = split(kernel_ref[0])
        high_ref[lag] = high
        low_ref[lag] = low

        @pl.when(lag == 0)
        def _():
            first_high_ref[...] = high
            first_low_ref[...] = low

    out = pltpu.VMEM(kernel.shape, BF16)
    first = pltpu.VMEM(kernel.shape[1:], BF16)
    return pl.pallas_call(
        body,
        grid=(lag_dev,),
        out_shape=(out, out, first, first),
        in_specs=[pl.BlockSpec((1, near, size, size), lambda lag: (lag, 0, 0, 0))],
        out_specs=(VMEM,) * 4,
        compiler_params=PARAMS,
        name="split_kernel",
    )(kernel)


def near_partial(near_t, base, received, high, low, copies):
    lag_dev, near, size, _ = high.shape
    peers, steps, _, waves, _ = received.shape

    def body(near_ref, base_ref, received_ref, high_ref, low_ref, out_ref, rest_ref):
        total = jnp.zeros((steps * waves, size), F32)
        for lag in range(lag_dev):
            for slot in range(near):
                source = jnp.bitwise_xor(near_ref[slot, 0, lag], base_ref[0])
                peer, plane = source % peers, source // peers
                block = jnp.concatenate([received_ref[peer, step, plane] for step in range(steps)], axis=0)
                total = total + product(block, high_ref[lag, slot], low_ref[lag, slot])
        for copy in range(copies):
            out_ref[copy] = total[:waves]
        rest_ref[...] = total[waves:]

    out = (pltpu.VMEM((copies, waves, size), F32), pltpu.VMEM((waves, size), F32))
    return call(body, out, [SMEM, SMEM] + [VMEM] * 3, [near_t, base, received, high, low])


def first_density(base, partials, incident, twin_incident, inverse, twin_inverse, chips, peers):
    groups = partials.shape[0] // 2
    waves, size = twin_incident.shape

    def body(base_ref, partials_ref, inc_ref, twin_inc_ref, inv_ref, twin_inv_ref, out_ref):
        own = (base_ref[0] // peers) * groups
        twin = groups - own
        near = partials_ref[own]
        twin_near = partials_ref[twin]
        for group in range(1, groups):
            near = near + partials_ref[own + group]
            twin_near = twin_near + partials_ref[twin + group]
        density = product(inc_ref[0] - near, *split(inv_ref[...]))
        twin_density = product(twin_inc_ref[...] - twin_near, *split(twin_inv_ref[...]))
        for chip in range(chips):
            out_ref[chip, 0] = density
            out_ref[chip, 1] = twin_density

    out = pltpu.VMEM((chips, 2, waves, size), F32)
    operands = [base, partials, incident, twin_incident, inverse, twin_inverse]
    return call(body, out, [SMEM] + [VMEM] * 5, operands)


def last_density(near_t, base, core, mine, partner, high, low, driven, inverse):
    near = near_t.shape[0]
    waves, size = driven.shape
    chips = mine.shape[0]

    def body(near_ref, base_ref, core_ref, mine_ref, partner_ref, high_ref, low_ref, driven_ref, inv_ref, out_ref):
        total = jnp.zeros((waves, size), F32)
        for slot in range(near):
            source = jnp.bitwise_xor(near_ref[slot, 0, 0], base_ref[0])
            chip = (source // 2) % chips
            plane = source // (2 * chips)
            same = (source % 2) == core_ref[0]
            block = jnp.where(same, mine_ref[chip, plane], partner_ref[chip, plane])
            total = total + product(block, high_ref[slot], low_ref[slot])
        out_ref[...] = product(driven_ref[...] - total, *split(inv_ref[...]))

    out = pltpu.VMEM((waves, size), F32)
    operands = [near_t, base, core, mine, partner, high, low, driven, inverse]
    return call(body, out, [SMEM] * 3 + [VMEM] * 6, operands)


def shards(history, incident, kernel, near_blocks, self_inverse):
    lag_dev, _, size = history.shape
    inverse = self_inverse[0]
    planes = lax.axis_size("z_hi")
    peers = lax.axis_size(PLANE)
    chips = peers // 2
    groups = lax.axis_size("lags")
    plane = lax.axis_index("z_hi")
    core = lax.axis_index("core")[None]
    base = (plane * peers)[None]
    near_t = jnp.transpose(near_blocks, (2, 0, 1))
    swap = [(0, 1), (1, 0)]

    def exchange(array, axes):
        return lax.all_to_all(array, axes, 0, 0, tiled=True)

    table = lag_table(near_t, base, peers, 128)
    table = exchange(table[:, None, :], PLANE)
    twin = lax.ppermute(history, "z_hi", swap)

    edge = history[lag_dev - 1]
    before = lax.ppermute(edge, "lags", [(g, g + 1) for g in range(groups - 1)])
    crossing = [(p * groups + g, (1 - p) * groups + g + 1) for p in range(planes) for g in range(groups - 1)]
    twin_before = lax.ppermute(edge, ("z_hi", "lags"), crossing)
    aside = lax.ppermute(jnp.concatenate([inverse, incident[0]], axis=0), "z_hi", swap)
    twin_inverse, twin_incident = aside[:size], aside[size:]

    received = exchange(pack(table, history, twin, before, twin_before), PLANE)
    high, low, first_high, first_low = split_kernel(kernel[0])
    partial0, partial1 = near_partial(near_t, base, received, high, low, planes * groups)

    partials = exchange(partial0, ("z_hi", "lags"))
    density0 = first_density(base, partials, incident, twin_incident, inverse, twin_inverse, chips, peers)
    mine = exchange(density0, ("y", "x"))
    partner = lax.ppermute(mine, "core", swap)

    driven = incident[1] - partial1
    for group in range(1, groups):
        driven = driven - lax.ppermute(partial1, "lags", [(group, 0)])

    density1 = last_density(near_t, base, core, mine, partner, first_high, first_low, driven, inverse)
    result = jnp.where(lax.axis_index("lags") == 0, density1, 0.0)
    for group in range(1, groups):
        result = result + lax.ppermute(density1, "lags", [(0, group)])
    return jnp.stack([density0[0, 0], result])


def solution(mesh):
    shape = (2, 4, 4, 2, mesh.shape["lags"])
    parts = Mesh(mesh.devices.reshape(shape), ROWS + ("lags",))
    in_specs = (
        P("lags", None, ROWS),
        P(None, None, ROWS),
        P(ROWS, "lags", None, None, None),
        P(ROWS, "lags", None),
        P(ROWS, None, None),
    )
    out_specs = P(None, None, ROWS)
    return jax.shard_map(shards, mesh=parts, in_specs=in_specs, out_specs=out_specs, check_vma=False)
```

```python
import jax
import jax.numpy as jnp
from jax import lax
from jax.experimental import pallas as pl
from jax.experimental.pallas import tpu as pltpu
from jax.sharding import Mesh
from jax.sharding import PartitionSpec as P


PLANE = ("y", "x", "core")
ROWS = ("z_hi",) + PLANE
F32 = jnp.float32
BF16 = jnp.bfloat16
VMEM = pl.BlockSpec(memory_space=pltpu.VMEM)
SMEM = pl.BlockSpec(memory_space=pltpu.SMEM)
PARAMS = pltpu.CompilerParams(vmem_limit_bytes=8 << 20)


def resident(array):
    return pltpu.with_memory_space_constraint(array, pltpu.VMEM)


def call(body, out, in_specs, operands, aliases=None):
    held = [resident(a) if s is VMEM else a for a, s in zip(operands, in_specs)]
    return pl.pallas_call(
        body,
        out_shape=out,
        in_specs=in_specs,
        out_specs=jax.tree.map(lambda _: VMEM, out),
        input_output_aliases=aliases or {},
        compiler_params=PARAMS,
    )(*held)


def split(value):
    high = value.astype(BF16)
    low = (value - high.astype(F32)).astype(BF16)
    return high, low


def product(left, right_high, right_low):
    waves = left.shape[0]
    left_high, left_low = split(left)
    both = jnp.concatenate([left_high, left_low], axis=0)
    first = jnp.dot(both, right_high, preferred_element_type=F32)
    second = jnp.dot(left_high, right_low, preferred_element_type=F32)
    return first[:waves] + (first[waves:] + second)


def lag_table(near_t, place, peers, lanes):
    near, _, lag_dev = near_t.shape

    def body(near_ref, place_ref, out_ref):
        ids = lax.broadcasted_iota(jnp.int32, (peers, lanes), 1) * peers
        ids = ids + lax.broadcasted_iota(jnp.int32, (peers, lanes), 0)
        table = jnp.zeros((peers, lanes), jnp.int32)
        for slot in range(near):
            for lag in range(1, lag_dev):
                source = jnp.bitwise_xor(near_ref[slot, 0, lag], place_ref[0])
                table = jnp.where(ids == source, lag, table)
        out_ref[...] = table

    return call(body, jax.ShapeDtypeStruct((peers, lanes), jnp.int32), [SMEM, SMEM], [near_t, place])


def stage(history):
    def body(history_ref, out_ref):
        out_ref[...] = history_ref[...]

    return pl.pallas_call(
        body,
        out_shape=pltpu.VMEM(history.shape, F32),
        out_specs=VMEM,
        compiler_params=PARAMS,
        name="stage",
    )(pltpu.with_memory_space_constraint(history, pltpu.HBM))


def pack(table, own, twin):
    peers, _, _ = table.shape
    block = own.shape[1:]
    part = peers // 4

    def body(table_ref, own_ref, twin_ref, out_ref):
        for step in range(part):
            peer = pl.program_id(0) * part + step
            for plane, ref in enumerate((own_ref, twin_ref)):
                lag = table_ref[peer, 0, plane]
                out_ref[step, 0, plane] = ref[lag]
                out_ref[step, 1, plane] = ref[jnp.maximum(lag - 1, 0)]

    return pl.pallas_call(
        body,
        grid=(peers // part,),
        out_shape=pltpu.HBM((peers, 2, 2) + block, F32),
        in_specs=[SMEM, VMEM, VMEM],
        out_specs=pl.BlockSpec((part, 2, 2) + block, lambda step: (step, 0, 0, 0, 0)),
        compiler_params=PARAMS,
        name="pack",
    )(table, resident(own), resident(twin))


def split_kernel(kernel):
    lag_dev, near, size, _ = kernel.shape

    def body(kernel_ref, high_ref, low_ref):
        high, low = split(kernel_ref[0])
        high_ref[0] = high
        low_ref[0] = low

    spec = pl.BlockSpec((1, near, size, size), lambda lag: (lag, 0, 0, 0))
    out = pltpu.HBM(kernel.shape, BF16)
    return pl.pallas_call(
        body,
        grid=(lag_dev,),
        out_shape=(out, out),
        in_specs=[spec],
        out_specs=(spec, spec),
        compiler_params=PARAMS,
        name="split_kernel",
    )(pltpu.with_memory_space_constraint(kernel, pltpu.HBM))


def near_partial(near_t, place, received, high, low, copies):
    lag_dev, near, size, _ = high.shape
    peers, steps, _, waves, _ = received.shape

    def body(near_ref, place_ref, received_ref, high_ref, low_ref, out_ref, rest_ref, total_ref):
        lag = pl.program_id(0)
        total = jnp.zeros((steps * waves, size), F32)
        for slot in range(near):
            source = jnp.bitwise_xor(near_ref[slot, 0, lag], place_ref[0])
            peer, plane = source % peers, source // peers
            later = jnp.where(lag == 0, 0.0, received_ref[peer, 1, plane])
            block = jnp.concatenate([received_ref[peer, 0, plane], later], axis=0)
            total = total + product(block, high_ref[0, slot], low_ref[0, slot])

        @pl.when(lag == 0)
        def _():
            total_ref[...] = total

        @pl.when(lag > 0)
        def _():
            total_ref[...] += total

        @pl.when(lag == lag_dev - 1)
        def _():
            for copy in range(copies):
                out_ref[copy] = total_ref[:waves]
            rest_ref[...] = total_ref[waves:]

    spec = pl.BlockSpec((1, near, size, size), lambda lag: (lag, 0, 0, 0))
    return pl.pallas_call(
        body,
        grid=(lag_dev,),
        out_shape=(
            jax.ShapeDtypeStruct((copies, waves, size), F32),
            jax.ShapeDtypeStruct((waves, size), F32),
        ),
        in_specs=[SMEM, SMEM, VMEM, spec, spec],
        out_specs=(VMEM, VMEM),
        scratch_shapes=[pltpu.VMEM((steps * waves, size), F32)],
        compiler_params=PARAMS,
        name="near",
    )(
        near_t,
        place,
        resident(received),
        pltpu.with_memory_space_constraint(high, pltpu.HBM),
        pltpu.with_memory_space_constraint(low, pltpu.HBM),
    )


def gather_twin(aside, before, twin_before, incident):
    waves, size = before.shape

    def body(aside_ref, before_ref, twin_before_ref, incident_ref, pair_ref, inverse_ref):
        pair_ref[0, 0] = incident_ref[0]
        pair_ref[0, 1] = aside_ref[size:]
        pair_ref[1, 0] = before_ref[...]
        pair_ref[1, 1] = twin_before_ref[...]
        inverse_ref[...] = aside_ref[:size]

    out = (pltpu.VMEM((2, 2, waves, size), F32), pltpu.VMEM((size, size), F32))
    return call(body, out, [VMEM] * 4, [aside, before, twin_before, incident])


def first_density(place, partials, pair, inverse, twin_inverse, chips, peers):
    groups = partials.shape[0] // 2
    waves, size = partials.shape[1:]

    def body(place_ref, partials_ref, pair_ref, inv_ref, twin_inv_ref, density_ref, out_ref):
        own = (place_ref[0] // peers) * groups
        twin = groups - own
        near = partials_ref[own]
        twin_near = partials_ref[twin]
        for group in range(1, groups):
            near = near + partials_ref[own + group]
            twin_near = twin_near + partials_ref[twin + group]
        density = product(pair_ref[0, 0] - near, *split(inv_ref[...]))
        twin_density = product(pair_ref[0, 1] - twin_near, *split(twin_inv_ref[...]))
        density_ref[...] = density
        new = place_ref[2] == 0
        first = jnp.where(new, density, pair_ref[1, 0])
        second = jnp.where(new, twin_density, pair_ref[1, 1])
        for chip in range(chips):
            out_ref[chip, 0] = first
            out_ref[chip, 1] = second

    out = (pltpu.VMEM((waves, size), F32), pltpu.VMEM((chips, 2, waves, size), F32))
    operands = [place, partials, pair, inverse, twin_inverse]
    return call(body, out, [SMEM] + [VMEM] * 4, operands)


def first_lag(near_t, place, mine, partner, high, low, rest):
    near = near_t.shape[0]
    chips = mine.shape[0]

    def body(near_ref, place_ref, mine_ref, partner_ref, high_ref, low_ref, rest_ref, out_ref):
        total = rest_ref[...]
        for slot in range(near):
            source = jnp.bitwise_xor(near_ref[slot, 0, 0], place_ref[0])
            chip = (source // 2) % chips
            plane = source // (2 * chips)
            same = (source % 2) == place_ref[1]
            block = jnp.where(same, mine_ref[chip, plane], partner_ref[chip, plane])
            total = total + product(block, high_ref[0, slot], low_ref[0, slot])
        out_ref[...] = total

    first = pl.BlockSpec((1,) + high.shape[1:], lambda step: (0, 0, 0, 0))
    return pl.pallas_call(
        body,
        grid=(1,),
        out_shape=pltpu.VMEM(rest.shape, F32),
        in_specs=[SMEM, SMEM, VMEM, VMEM, first, first, VMEM],
        out_specs=VMEM,
        compiler_params=PARAMS,
        name="first_lag",
    )(
        near_t,
        place,
        resident(mine),
        resident(partner),
        pltpu.with_memory_space_constraint(high, pltpu.HBM),
        pltpu.with_memory_space_constraint(low, pltpu.HBM),
        resident(rest),
    )


def last_density(place, partials, incident, inverse, density0):
    groups = len(partials)

    def body(place_ref, inc_ref, inv_ref, density_ref, *refs):
        terms, (out_ref, held_ref) = refs[:groups], refs[groups:]
        for ahead, term in enumerate(terms):
            held_ref[lax.rem(place_ref[2] - ahead + groups, groups)] = term[...]
        driven = inc_ref[1]
        for group in range(groups):
            driven = driven - held_ref[group]
        out_ref[0] = density_ref[...]
        out_ref[1] = product(driven, *split(inv_ref[...]))

    operands = [incident, inverse, density0, *partials]
    return pl.pallas_call(
        body,
        out_shape=jax.ShapeDtypeStruct((2,) + density0.shape, F32),
        in_specs=[SMEM] + [VMEM] * len(operands),
        out_specs=VMEM,
        scratch_shapes=[pltpu.VMEM((groups,) + density0.shape, F32)],
        compiler_params=PARAMS,
        name="last_density",
    )(place, *[resident(a) for a in operands])


def shards(history, incident, kernel, near_blocks, self_inverse):
    lag_dev, _, _ = history.shape
    inverse = self_inverse[0]
    planes = lax.axis_size("z_hi")
    peers = lax.axis_size(PLANE)
    chips = peers // 2
    groups = lax.axis_size("lags")
    place = jnp.stack([lax.axis_index("z_hi") * peers, lax.axis_index("core"), lax.axis_index("lags")])
    near_t = jnp.transpose(near_blocks, (2, 0, 1))
    swap = [(0, 1), (1, 0)]

    def exchange(array, axes):
        return lax.all_to_all(array, axes, 0, 0, tiled=True)

    table = lag_table(near_t, place, peers, 128)
    table = exchange(table[:, None, :], PLANE)
    twin = lax.ppermute(history, "z_hi", swap)
    received = exchange(pack(table, stage(history), twin), PLANE)

    edge = history[lag_dev - 1]
    before = lax.ppermute(edge, "lags", [(g, g + 1) for g in range(groups - 1)])
    crossing = [(p * groups + g, (1 - p) * groups + g + 1) for p in range(planes) for g in range(groups - 1)]
    twin_before = lax.ppermute(edge, ("z_hi", "lags"), crossing)
    aside = lax.ppermute(jnp.concatenate([inverse, incident[0]], axis=0), "z_hi", swap)
    pair, twin_inverse = gather_twin(aside, before, twin_before, incident)

    high, low = split_kernel(kernel[0])
    partial0, partial1 = near_partial(near_t, place, received, high, low, planes * groups)

    partials = exchange(partial0, ("z_hi", "lags"))
    density0, spread = first_density(place, partials, pair, inverse, twin_inverse, chips, peers)
    mine = exchange(spread, ("y", "x"))
    partner = lax.ppermute(mine, "core", swap)

    partial1 = first_lag(near_t, place, mine, partner, high, low, partial1)
    terms = [partial1]
    for ahead in range(1, groups):
        route = [(g, (g + ahead) % groups) for g in range(groups)]
        terms.append(lax.ppermute(partial1, "lags", route))
    return last_density(place, terms, incident, inverse, density0)


def solution(mesh):
    shape = (2, 4, 4, 2, mesh.shape["lags"])
    parts = Mesh(mesh.devices.reshape(shape), ROWS + ("lags",))
    in_specs = (
        P("lags", None, ROWS),
        P(None, None, ROWS),
        P(ROWS, "lags", None, None, None),
        P(ROWS, "lags", None),
        P(ROWS, None, None),
    )
    out_specs = P(None, None, ROWS)
    return jax.shard_map(shards, mesh=parts, in_specs=in_specs, out_specs=out_specs, check_vma=False)
```
